256 devices in a mesh: row: 16 (over x_hi, z), col: 16 (over x_lo, y, core).
Axes of the slice: x: 4 (x_hi: 2, x_lo: 2; x = x_hi * 2 + x_lo), y: 4, z: 8, core: 2. Of those that a mesh axis runs over, the one named last changes fastest.
Arguments:
- log_rate: float32 [1048576], P(('row', 'col')), may hold values from -0.5 to 1
- state: float32 [1048576], P(('row', 'col')), may hold values from 0.2 to 1
- excess: float32 [1048576], P(('row', 'col')), may hold values from -0.3 to 0.3
- normal_stress: float32 [1048576], P(('row', 'col')), may hold values from 2 to 4
- rate_param: float32 [1048576], P(('row', 'col')), may hold values from 0.5 to 1
- state_param: float32 [1048576], P(('row', 'col')), may hold values from 0.5 to 1.5
- slip_length: float32 [1048576], P(('row', 'col')), may hold values from 1 to 4
- self_stiffness: float32 [1048576], P(('row', 'col')), may hold values from 0.2 to 1
- damping: float32 [1048576], P(('row', 'col')), may hold values from 1 to 2
- blocks: bfloat16 [16, 16, 512, 4096], P('row', 'col'), may hold values from -0.1796875 to 0.1796875
- pattern: int32 [16, 16, 512, 2], P('row', 'col'), may hold values from 0 to 1023, as said below
- counts: int32 [16, 16], P('row', 'col'), may hold values from 1 to 512, as said below
Outputs:
- final_log_rate: float32 [1048576], P(('row', 'col'))
- final_state: float32 [1048576], P(('row', 'col'))
- final_stress: float32 [1048576], P(('row', 'col'))
The draws below stay inside these ranges and needn't reach their ends.
Inputs may be any that keep to these rules, and one draw needn't show every extreme that they name: Each slot (i, j) has global block row I no larger than global block column J (upper pattern, I and J as in the reference program); the same position may be stored in several slots, whose tiles then add; slots at or past the device's count hold valid indices that are ignored. `counts`: every device holds at least one live tile; some device of the first index of row holds 512.
All inputs are finite; a program needn't handle non-finite values.
Results may differ from the reference program's by a relative error of at most 0.0014.
Values may be sent and summed in bfloat16 or wider, within the bound.
No kernel may reach another device: no remote copies, remote signals or barrier semaphores. Data moves between devices by JAX's collectives and lax.ppermute only.
A program may use at most 64 MiB of HBM per device.

```python
import math
import jax
import jax.numpy as jnp
from jax import lax

PATCH_DEV = 4096
NB_DEV = 512
STEPS = 2
NEWTON = 4
PATCHES = 1048576
N_ROW = 16
N_COL = 16


def block_layout(key):
    key = jax.random.fold_in(key, 4242)
    keys = jax.random.split(key, 5)
    per_seg = PATCH_DEV // 64
    shape = (N_ROW, N_COL, NB_DEV)
    row_ids = jnp.arange(N_ROW, dtype=jnp.int32)
    col_ids = jnp.arange(N_COL, dtype=jnp.int32)
    top_load = jnp.maximum(1, NB_DEV * (N_ROW - row_ids) // N_ROW)
    top_load = jnp.broadcast_to(top_load[:, None], (N_ROW, N_COL))
    low_load = jnp.maximum(1, top_load // 2)
    loads = jax.random.randint(keys[0], (N_ROW, N_COL), low_load, top_load + 1)
    busiest = jax.random.randint(keys[1], (), 0, N_COL)
    heavy = (row_ids[:, None] == 0) & (col_ids[None, :] == busiest)
    loads = jnp.where(heavy, NB_DEV, loads)
    rows_b = jnp.broadcast_to(row_ids[:, None, None], shape)
    cols_b = jnp.broadcast_to(col_ids[None, :, None], shape)
    far_row = jax.random.randint(keys[2], shape, rows_b, N_ROW)
    offset = jax.random.randint(keys[3], shape, 0, per_seg)
    raw_row = jax.random.randint(keys[4], shape, 0, N_COL * per_seg)
    limit_row = cols_b * per_seg + offset
    bad = (far_row == rows_b) & (raw_row > limit_row)
    row_slot = jnp.where(bad, raw_row % (limit_row + 1), raw_row)
    col_slot = far_row * per_seg + offset
    pattern = jnp.stack([row_slot, col_slot], axis=-1).astype(jnp.int32)
    return (pattern, loads.astype(jnp.int32))


def draw_pattern(key, part):
    return block_layout(key)[0]


def draw_counts(key, part):
    return block_layout(key)[1]


def block_levels(key, extent, cuts, smallest, top_value):
    level = 1.0
    for dim, shards_of in cuts:
        heights = jax.random.uniform(jax.random.fold_in(jax.random.fold_in(key, 6), dim), (shards_of,), jnp.float32, smallest / len(cuts), top_value / len(cuts))
        level = level * jnp.repeat(jnp.exp(heights), extent[dim] // shards_of).reshape((-1,) + (1,) * (len(extent) - 1 - dim))
    return level


def centred(stream_key, extent, width, reach, cuts=(), held_as=jnp.bfloat16):
    gain = block_levels(stream_key, extent, cuts, -0.22, 0.18) if cuts else 1.0
    result = jax.random.normal(stream_key, extent, jnp.float32) * width * gain
    return jnp.minimum(jnp.maximum(result, -reach), reach).astype(held_as)


def setup_inputs(seed: int = 0) -> dict:
    streams_of = jax.random.split(jax.random.key(seed), 13)
    return {
        "log_rate": jnp.clip(-0.5 + 1.5 * jax.random.uniform(streams_of[0], (PATCHES,), jnp.float32) ** block_levels(streams_of[0], (PATCHES,), ((0, 256),), -0.2, 0.2), -0.5, 1.0),
        "state": jnp.clip(0.2 + 0.8 * jax.random.uniform(streams_of[1], (PATCHES,), jnp.float32) ** block_levels(streams_of[1], (PATCHES,), ((0, 256),), -0.2, 0.2), 0.2, 1.0),
        "excess": jnp.clip(jax.random.uniform(streams_of[2], (PATCHES,), jnp.float32, -0.3, 0.3) * block_levels(streams_of[2], (PATCHES,), ((0, 256),), -0.4, 0.0), -0.3, 0.3),
        "normal_stress": jnp.clip(jnp.exp(math.log(4.0) - 0.6931472 * jax.random.uniform(streams_of[3], (PATCHES,), jnp.float32) ** block_levels(streams_of[3], (PATCHES,), ((0, 256),), -0.2, 0.2)), 2.0, 4.0),
        "rate_param": jnp.clip(jnp.exp(math.log(1.0) - 0.6931472 * jax.random.uniform(streams_of[4], (PATCHES,), jnp.float32) ** block_levels(streams_of[4], (PATCHES,), ((0, 256),), -0.2, 0.2)), 0.5, 1.0),
        "state_param": jnp.clip(jnp.exp(math.log(1.5) - 1.0986123 * jax.random.uniform(streams_of[5], (PATCHES,), jnp.float32) ** block_levels(streams_of[5], (PATCHES,), ((0, 256),), -0.2, 0.2)), 0.5, 1.5),
        "slip_length": jnp.clip(jnp.exp(math.log(4.0) - 1.3862944 * jax.random.uniform(streams_of[6], (PATCHES,), jnp.float32) ** block_levels(streams_of[6], (PATCHES,), ((0, 256),), -0.2, 0.2)), 1.0, 4.0),
        "self_stiffness": jnp.clip(jnp.exp(math.log(1.0) - 1.609438 * jax.random.uniform(streams_of[7], (PATCHES,), jnp.float32) ** block_levels(streams_of[7], (PATCHES,), ((0, 256),), -0.2, 0.2)), 0.2, 1.0),
        "damping": jnp.clip(jnp.exp(math.log(2.0) - 0.6931472 * jax.random.uniform(streams_of[8], (PATCHES,), jnp.float32) ** block_levels(streams_of[8], (PATCHES,), ((0, 256),), -0.2, 0.2)), 1.0, 2.0),
        "blocks": centred(streams_of[9], (N_ROW, N_COL, NB_DEV, 4096), 0.03, 0.1796875, ((0, 16), (1, 16))),
        "pattern": draw_pattern(jax.random.fold_in(streams_of[12], 71), 0),
        "counts": draw_counts(jax.random.fold_in(streams_of[12], 71), 0),
    }


time_step = 0.25

def inverse_sinh(value):
    return jnp.log(value + jnp.sqrt(1.0 + value * value))

def apply_kernel(pushed, blocks, pattern, counts):
    per_seg = PATCH_DEV // 64
    pieces = pushed.astype(jnp.float32).reshape(-1, 64)
    tiles_all = blocks.reshape(N_ROW * N_COL, NB_DEV, 64, 64)
    places_all = pattern.reshape(N_ROW * N_COL, NB_DEV, 2)
    stored_all = counts.reshape(-1)

    def visit(stress_rate, inputs):
        device, kernel_tiles, places, stored = inputs
        my_row = device // N_COL
        my_col = device % N_COL
        row_slot = places[:, 0]
        col_slot = places[:, 1]
        global_row = (my_row * N_COL * per_seg + row_slot).astype(jnp.int32)
        global_col = ((col_slot // per_seg * N_COL + my_col) * per_seg + col_slot % per_seg).astype(jnp.int32)
        active = jnp.arange(NB_DEV, dtype=jnp.int32) < stored
        dense_tiles = kernel_tiles.astype(jnp.float32)
        direct = jnp.einsum('bij,bj->bi', dense_tiles, pieces[global_col], precision=lax.Precision.HIGHEST)
        mirror = jnp.einsum('bij,bi->bj', dense_tiles, pieces[global_row], precision=lax.Precision.HIGHEST)
        direct = jnp.where(active[:, None], direct, 0.0)
        mirror = jnp.where((active & (global_row != global_col))[:, None], mirror, 0.0)
        stress_rate = stress_rate.at[global_row].add(direct).at[global_col].add(mirror)
        return (stress_rate, None)
    start = jnp.zeros(pieces.shape, jnp.float32)
    stress_rate, unused = lax.scan(visit, start, (jnp.arange(N_ROW * N_COL, dtype=jnp.int32), tiles_all, places_all, stored_all))
    return stress_rate.reshape(-1)

def friction_solve(rate_log, stress, state, normal_stress, rate_param, damping):
    for turn_index in range(NEWTON):
        speed = jnp.exp(rate_log)
        ratio = 0.5 * jnp.exp(rate_log + state / rate_param)
        misfit = stress - damping * speed - normal_stress * rate_param * inverse_sinh(ratio)
        slope = -damping * speed - normal_stress * rate_param * ratio / jnp.sqrt(1.0 + ratio * ratio)
        rate_log = rate_log - misfit / slope
    return rate_log

def reference(log_rate, state, excess, normal_stress, rate_param, state_param, slip_length, self_stiffness, damping, blocks, pattern, counts):
    rate_log = log_rate
    balance = normal_stress * rate_param * inverse_sinh(0.5 * jnp.exp(log_rate + state / rate_param)) + damping * jnp.exp(log_rate)
    stress = balance * (1.0 + excess)
    for step_index in range(STEPS):
        speed = jnp.exp(rate_log)
        pushed = (speed - 1.0).astype(jnp.bfloat16)
        stress_rate = apply_kernel(pushed, blocks, pattern, counts)
        new_stress = stress + time_step * (stress_rate - self_stiffness * (speed - 1.0))
        state = state + time_step * (state_param / slip_length) * (jnp.exp(-state / state_param) - speed)
        stress = new_stress
        rate_log = friction_solve(rate_log, stress, state, normal_stress, rate_param, damping)
    return (rate_log, state, stress)
```

```python
import functools

import jax
import jax.numpy as jnp
from jax import lax
from jax.experimental import pallas as pl
from jax.experimental.pallas import tpu as pltpu
from jax.sharding import PartitionSpec as P

STEPS = 2
NEWTON = 4
TILE = 64
LANES = 128
CHUNK = 128

time_step = 0.25


def inverse_sinh(value):
    return jnp.log(value + jnp.sqrt(1.0 + value * value))


def friction_solve(rate_log, stress, state, normal_stress, rate_param, damping):
    strength = normal_stress * rate_param
    lift = state / rate_param
    for turn_index in range(NEWTON):
        speed = jnp.exp(rate_log)
        ratio = 0.5 * jnp.exp(rate_log + lift)
        root = jnp.sqrt(1.0 + ratio * ratio)
        misfit = stress - damping * speed - strength * jnp.log(ratio + root)
        slope = -damping * speed - strength * ratio / root
        rate_log = rate_log - misfit / slope
    return rate_log


def start_kernel(log_rate, state, excess, normal_stress, rate_param, damping, stress_out, pushed_out):
    speed = jnp.exp(log_rate[...])
    balance = normal_stress[...] * rate_param[...] * inverse_sinh(
        0.5 * jnp.exp(log_rate[...] + state[...] / rate_param[...])
    ) + damping[...] * speed
    stress_out[...] = balance * (1.0 + excess[...])
    pushed = (speed - 1.0).astype(jnp.bfloat16)
    pushed_out[...] = jnp.broadcast_to(pushed[None], pushed_out.shape)


def step_kernel(
    direct,
    mirror,
    rate_log,
    stress,
    state,
    normal_stress,
    rate_param,
    state_param,
    slip_length,
    self_stiffness,
    damping,
    rate_out,
    state_out,
    stress_out,
    *pushed_out,
):
    stress_rate = jnp.sum(direct[...].astype(jnp.float32), axis=0) + jnp.sum(
        mirror[...].astype(jnp.float32), axis=0
    )
    speed = jnp.exp(rate_log[...])
    old_state = state[...]
    new_stress = stress[...] + time_step * (stress_rate - self_stiffness[...] * (speed - 1.0))
    new_state = old_state + time_step * (state_param[...] / slip_length[...]) * (
        jnp.exp(-old_state / state_param[...]) - speed
    )
    new_rate = friction_solve(
        rate_log[...], new_stress, new_state, normal_stress[...], rate_param[...], damping[...]
    )
    rate_out[...] = new_rate
    state_out[...] = new_state
    stress_out[...] = new_stress
    for out in pushed_out:
        pushed = (jnp.exp(new_rate) - 1.0).astype(jnp.bfloat16)
        out[...] = jnp.broadcast_to(pushed[None], out.shape)


def pick_half(values, odd):
    lane = lax.broadcasted_iota(jnp.int32, values.shape, 1)
    return jnp.where((lane < TILE) == (odd == 0), values, pltpu.roll(values, TILE, 1))


def place_half(values, odd):
    lane = lax.broadcasted_iota(jnp.int32, values.shape, 1)
    return jnp.where((lane < TILE) == (odd == 0), values, 0.0)


def product_kernel(
    tiles, across, down, down_mirror, row_rates, col_rates, spread, gather, row_out, col_out, row_acc, col_acc
):
    chunk = pl.program_id(0)

    @pl.when(chunk == 0)
    def _():
        row_acc[...] = jnp.zeros_like(row_acc)
        col_acc[...] = jnp.zeros_like(col_acc)

    pairs = row_rates.shape[0]
    bf16 = jnp.bfloat16
    row_slot = across[:, 0:1]
    col_slot = across[:, 1:2]
    wide = lax.broadcasted_iota(jnp.int32, (CHUNK, pairs), 1)
    row_pick = jnp.where(wide == row_slot // 2, 1.0, 0.0).astype(bf16)
    col_pick = jnp.where(wide == col_slot // 2, 1.0, 0.0).astype(bf16)
    tall = lax.broadcasted_iota(jnp.int32, (pairs, CHUNK), 0)
    row_drop = jnp.where(tall == down[0:1, :], 1.0, 0.0).astype(bf16)
    col_drop = jnp.where(tall == down_mirror[0:1, :], 1.0, 0.0).astype(bf16)

    col_piece = jnp.dot(col_pick, col_rates[...], preferred_element_type=jnp.float32)
    row_piece = jnp.dot(row_pick, row_rates[...], preferred_element_type=jnp.float32)
    col_piece = pick_half(col_piece, col_slot % 2).astype(bf16)
    row_piece = pick_half(row_piece, row_slot % 2).astype(bf16)

    direct = jnp.zeros((CHUNK, LANES), jnp.float32)
    mirror = jnp.zeros((CHUNK, LANES), jnp.float32)
    width = 2 * LANES
    col_wide = jnp.concatenate([col_piece, col_piece], axis=1)
    for part in range(tiles.shape[1] // width):
        lanes = pl.ds(part * width, width)
        tile = tiles[:, lanes]
        direct += jnp.dot(tile * col_wide, gather[lanes, :], preferred_element_type=jnp.float32)
        spread_rate = jnp.dot(row_piece, spread[:, lanes], preferred_element_type=jnp.float32)
        product = tile.astype(jnp.float32) * spread_rate
        mirror += product[:, :LANES] + product[:, LANES:]
    mirror = mirror + pltpu.roll(mirror, TILE, 1)
    direct = place_half(direct, row_slot % 2).astype(bf16)
    mirror = place_half(mirror, col_slot % 2).astype(bf16)
    row_acc[...] += jnp.dot(row_drop, direct, preferred_element_type=jnp.float32)
    col_acc[...] += jnp.dot(col_drop, mirror, preferred_element_type=jnp.float32)

    @pl.when(chunk == pl.num_programs(0) - 1)
    def _():
        row_out[...] = row_acc[...].astype(bf16)
        col_out[...] = col_acc[...].astype(bf16)


def on_device(
    log_rate,
    state,
    excess,
    normal_stress,
    rate_param,
    state_param,
    slip_length,
    self_stiffness,
    damping,
    blocks,
    pattern,
    counts,
):
    patches = log_rate.shape[0]
    per_seg = patches // TILE
    my_row = lax.axis_index("row")
    my_col = lax.axis_index("col")
    row_count = lax.axis_size("row")
    col_count = lax.axis_size("col")
    slots = blocks.shape[2]
    tile_size = blocks.shape[3]
    flat = (patches // LANES, LANES)
    bf16 = jnp.bfloat16
    f32 = jnp.float32

    kernel_tiles = blocks.reshape(slots, tile_size)
    places = pattern.reshape(slots, 2)
    row_slot = places[:, 0]
    col_slot = places[:, 1]
    live = jnp.arange(slots, dtype=jnp.int32) < counts[0, 0]
    diagonal = (col_slot // per_seg == my_row) & (row_slot == my_col * per_seg + col_slot % per_seg)
    across = jnp.where(live[:, None], places, -2)
    down = jnp.where(live, row_slot // 2, -1)[None]
    down_mirror = jnp.where(live & jnp.logical_not(diagonal), col_slot // 2, -1)[None]
    entry = jnp.arange(tile_size, dtype=jnp.int32)
    lane = jnp.arange(LANES, dtype=jnp.int32)
    spread = (entry[None, :] // TILE == lane[:, None]).astype(bf16)
    gather = (entry[:, None] // TILE == lane[None, :] % TILE).astype(bf16)

    whole = [a.reshape(flat) for a in (normal_stress, rate_param, state_param, slip_length, self_stiffness, damping)]
    normal_stress, rate_param, state_param, slip_length, self_stiffness, damping = whole
    rate_log = log_rate.reshape(flat)
    state = state.reshape(flat)
    group = (row_count,) + flat

    stress, pushed = pl.pallas_call(
        start_kernel,
        out_shape=(jax.ShapeDtypeStruct(flat, f32), jax.ShapeDtypeStruct(group, bf16)),
    )(rate_log, state, excess.reshape(flat), normal_stress, rate_param, damping)

    def exchange(x, axis):
        return lax.all_to_all(x, axis, split_axis=0, concat_axis=0, tiled=True)

    row_pairs = col_count * per_seg // 2
    col_pairs = row_count * per_seg // 2
    product = pl.pallas_call(
        product_kernel,
        grid=(slots // CHUNK,),
        in_specs=[
            pl.BlockSpec((CHUNK, tile_size), lambda i: (i, 0)),
            pl.BlockSpec((CHUNK, 2), lambda i: (i, 0)),
            pl.BlockSpec((1, CHUNK), lambda i: (0, i)),
            pl.BlockSpec((1, CHUNK), lambda i: (0, i)),
            pl.BlockSpec((row_pairs, LANES), lambda i: (0, 0)),
            pl.BlockSpec((col_pairs, LANES), lambda i: (0, 0)),
            pl.BlockSpec((LANES, tile_size), lambda i: (0, 0)),
            pl.BlockSpec((tile_size, LANES), lambda i: (0, 0)),
        ],
        out_specs=[
            pl.BlockSpec((row_pairs, LANES), lambda i: (0, 0)),
            pl.BlockSpec((col_pairs, LANES), lambda i: (0, 0)),
        ],
        out_shape=(
            jax.ShapeDtypeStruct((row_pairs, LANES), bf16),
            jax.ShapeDtypeStruct((col_pairs, LANES), bf16),
        ),
        scratch_shapes=[pltpu.VMEM((row_pairs, LANES), f32), pltpu.VMEM((col_pairs, LANES), f32)],
    )
    for step_index in range(STEPS):
        last = step_index == STEPS - 1
        row_rates = exchange(pushed, "col")
        col_rates = exchange(pushed, "row")
        row_total, col_total = product(
            kernel_tiles,
            across,
            down,
            down_mirror,
            row_rates.reshape(row_pairs, LANES),
            col_rates.reshape(col_pairs, LANES),
            spread,
            gather,
        )
        direct = exchange(row_total.reshape((col_count,) + flat), "col")
        mirror = exchange(col_total.reshape((row_count,) + flat), "row")
        outs = [jax.ShapeDtypeStruct(flat, f32)] * 3
        if not last:
            outs.append(jax.ShapeDtypeStruct(group, bf16))
        result = pl.pallas_call(step_kernel, out_shape=tuple(outs))(
            direct,
            mirror,
            rate_log,
            stress,
            state,
            normal_stress,
            rate_param,
            state_param,
            slip_length,
            self_stiffness,
            damping,
        )
        rate_log, state, stress = result[:3]
        if not last:
            pushed = result[3]
    return tuple(a.reshape(patches) for a in (rate_log, state, stress))


def solution(mesh):
    in_specs = (P(("row", "col")),) * 9 + (
        P("row", "col", None, None),
        P("row", "col", None, None),
        P("row", "col"),
    )
    out_specs = (P(("row", "col")), P(("row", "col")), P(("row", "col")))
    return jax.shard_map(
        on_device, mesh=mesh, in_specs=in_specs, out_specs=out_specs, check_vma=False
    )
```

```python
import jax
import jax.numpy as jnp
from jax import lax
from jax.experimental import pallas as pl
from jax.experimental.pallas import tpu as pltpu
from jax.sharding import PartitionSpec as P

STEPS = 2
NEWTON = 4
TILE = 64
LANES = 128
WIDTH = 256
ROWS = 128

time_step = 0.25
bf16 = jnp.bfloat16
f32 = jnp.float32


def friction_solve(rate_log, stress, state, normal_stress, rate_param, damping):
    strength = normal_stress * rate_param
    lift = state / rate_param
    for turn_index in range(NEWTON):
        speed = jnp.exp(rate_log)
        ratio = 0.5 * jnp.exp(rate_log + lift)
        root = jnp.sqrt(1.0 + ratio * ratio)
        misfit = stress - damping * speed - strength * jnp.log(ratio + root)
        slope = -damping * speed - strength * ratio / root
        rate_log = rate_log - misfit / slope
    return rate_log


def push_kernel(log_rate, pushed_out):
    pushed = (jnp.exp(log_rate[...]) - 1.0).astype(bf16)
    pushed_out[...] = jnp.broadcast_to(pushed[None], pushed_out.shape)


def as_column(row):
    wide = jnp.broadcast_to(row.astype(f32), (LANES, row.shape[1]))
    return jnp.transpose(wide).astype(jnp.int32)


def plan_kernel(
    places, counts, row_pick, col_pick, row_drop, col_drop, row_half, col_half, spread, gather
):
    slots = places.shape[1]
    row_slot = places[0:1, :]
    col_slot = places[1:2, :]
    segment = row_drop.shape[0] * 2 // lax.axis_size("col")
    my_row = lax.axis_index("row")
    my_col = lax.axis_index("col")
    live = lax.broadcasted_iota(jnp.int32, (1, slots), 1) < counts[0, 0]
    diagonal = (col_slot // segment == my_row) & (row_slot == my_col * segment + col_slot % segment)
    row_live = jnp.where(live, row_slot, -2)
    col_live = jnp.where(live, col_slot, -2)
    col_twin = jnp.where(live & jnp.logical_not(diagonal), col_slot, -2)

    for drop, index in ((row_drop, row_live), (col_drop, col_twin)):
        tall = lax.broadcasted_iota(jnp.int32, drop.shape, 0)
        drop[...] = jnp.where(tall == (index >> 1), 1.0, 0.0).astype(bf16)
    for pick, half, index in ((row_pick, row_half, row_live), (col_pick, col_half, col_live)):
        column = as_column(index)
        pair = column >> 1
        lane = lax.broadcasted_iota(jnp.int32, column.shape, 1)
        for start in range(0, pick.shape[1], LANES):
            pick[:, start : start + LANES] = jnp.where(pair == lane + start, 1.0, 0.0).astype(bf16)
        half[...] = jnp.where((lane < TILE) == ((column & 1) == 0), 1.0, 0.0)
    entry = lax.broadcasted_iota(jnp.int32, spread.shape, 1)
    spread[...] = jnp.where(
        entry // TILE == lax.broadcasted_iota(jnp.int32, spread.shape, 0), 1.0, 0.0
    ).astype(bf16)
    entry = lax.broadcasted_iota(jnp.int32, gather.shape, 0)
    gather[...] = jnp.where(
        entry // TILE == lax.broadcasted_iota(jnp.int32, gather.shape, 1) % TILE, 1.0, 0.0
    ).astype(bf16)


def chosen(pick, half, rates):
    both = jnp.dot(pick, rates, preferred_element_type=f32)
    return jnp.where(half > 0.5, both, pltpu.roll(both, TILE, 1)).astype(bf16)


def mirror_kernel(tiles, pick, row_half, col_half, drop, spread, rates, pushed, out, parts):
    rates = rates[...].reshape(-1, LANES)
    for base in range(0, tiles.shape[0], ROWS):
        rows = slice(base, base + ROWS)
        piece = chosen(pick[rows, :], row_half[rows, :], rates)
        total = jnp.zeros((ROWS, LANES), f32)
        for start in range(0, tiles.shape[1], WIDTH):
            wide = jnp.dot(piece, spread[:, start : start + WIDTH], preferred_element_type=f32)
            product = tiles[rows, start : start + WIDTH].astype(f32) * wide
            total += product[:, :LANES] + product[:, LANES:]
        total = total + pltpu.roll(total, TILE, 1)
        parts[rows, :] = (total * col_half[rows, :]).astype(bf16)
    sums = jnp.dot(drop[...], parts[...], preferred_element_type=f32)
    patches = pushed.shape[1]
    out[:, :patches, :] = sums.astype(bf16).reshape(pushed.shape)
    out[:, patches:, :] = pushed[...]


def direct_kernel(tiles, pick, col_half, row_half, drop, gather, got, out, parts):
    patches = out.shape[1]
    rates = got[:, patches:, :].reshape(-1, LANES)
    for base in range(0, tiles.shape[0], ROWS):
        rows = slice(base, base + ROWS)
        piece = chosen(pick[rows, :], col_half[rows, :], rates)
        piece = jnp.concatenate([piece] * (WIDTH // LANES), axis=1)
        total = jnp.zeros((ROWS, LANES), f32)
        for start in range(0, tiles.shape[1], WIDTH):
            total += jnp.dot(
                tiles[rows, start : start + WIDTH] * piece,
                gather[start : start + WIDTH, :],
                preferred_element_type=f32,
            )
        parts[rows, :] = (total * row_half[rows, :]).astype(bf16)
    sums = jnp.dot(drop[...], parts[...], preferred_element_type=f32)
    out[...] = sums.astype(bf16).reshape(out.shape)


def step_body(stress, direct, got, rate_log, state, more, outs):
    normal_stress, rate_param, state_param, slip_length, self_stiffness, damping = (m[...] for m in more)
    rate_out, state_out, stress_out, *pushed_out = outs
    stress_rate = jnp.sum(direct[...].astype(f32), axis=0) + jnp.sum(
        got[:, : direct.shape[1], :].astype(f32), axis=0
    )
    speed = jnp.exp(rate_log)
    new_stress = stress + time_step * (stress_rate - self_stiffness * (speed - 1.0))
    new_state = state + time_step * (state_param / slip_length) * (jnp.exp(-state / state_param) - speed)
    new_rate = friction_solve(rate_log, new_stress, new_state, normal_stress, rate_param, damping)
    rate_out[...] = new_rate
    state_out[...] = new_state
    stress_out[...] = new_stress
    for out in pushed_out:
        pushed = (jnp.exp(new_rate) - 1.0).astype(bf16)
        out[...] = jnp.broadcast_to(pushed[None], out.shape)


def first_kernel(direct, got, log_rate, state, excess, *refs):
    more, outs = refs[:6], refs[6:]
    normal_stress, rate_param, damping = more[0][...], more[1][...], more[5][...]
    rate_log, begin = log_rate[...], state[...]
    ratio = 0.5 * jnp.exp(rate_log + begin / rate_param)
    balance = normal_stress * rate_param * jnp.log(ratio + jnp.sqrt(1.0 + ratio * ratio)) + damping * jnp.exp(
        rate_log
    )
    step_body(balance * (1.0 + excess[...]), direct, got, rate_log, begin, more, outs)


def later_kernel(direct, got, rate_log, state, stress, *refs):
    step_body(stress[...], direct, got, rate_log[...], state[...], refs[:6], refs[6:])


def call(kernel, out_shape, scratch=(), **kw):
    return pl.pallas_call(
        kernel,
        out_shape=out_shape,
        scratch_shapes=list(scratch),
        compiler_params=pltpu.CompilerParams(vmem_limit_bytes=24 << 20),
        **kw,
    )


def on_device(
    log_rate,
    state,
    excess,
    normal_stress,
    rate_param,
    state_param,
    slip_length,
    self_stiffness,
    damping,
    blocks,
    pattern,
    counts,
):
    patches = log_rate.shape[0]
    flat = (patches // LANES, LANES)
    row_count = lax.axis_size("row")
    col_count = lax.axis_size("col")
    slots, tile_size = blocks.shape[2:]
    row_rows = col_count * flat[0]
    col_rows = row_count * flat[0]
    shape = jax.ShapeDtypeStruct

    tiles = blocks.reshape(slots, tile_size)
    places = pattern.reshape(slots, 2).T
    more = [
        a.reshape(flat)
        for a in (normal_stress, rate_param, state_param, slip_length, self_stiffness, damping)
    ]
    rate_log = log_rate.reshape(flat)
    state = state.reshape(flat)
    stress = excess.reshape(flat)
    vmem = pl.BlockSpec(memory_space=pltpu.VMEM)

    def exchange(x, axis):
        return lax.all_to_all(x, axis, split_axis=0, concat_axis=0, tiled=True)

    pushed = call(push_kernel, shape((col_count,) + flat, bf16))(rate_log)
    row_pick, col_pick, row_drop, col_drop, row_half, col_half, spread, gather = call(
        plan_kernel,
        (
            shape((slots, row_rows), bf16),
            shape((slots, col_rows), bf16),
            shape((row_rows, slots), bf16),
            shape((col_rows, slots), bf16),
            shape((slots, LANES), f32),
            shape((slots, LANES), f32),
            shape((LANES, tile_size), bf16),
            shape((tile_size, LANES), bf16),
        ),
        in_specs=[vmem, pl.BlockSpec(memory_space=pltpu.SMEM)],
    )(places, counts)
    parts = (pltpu.VMEM((slots, LANES), bf16),)
    for step_index in range(STEPS):
        row_rates = exchange(pushed, "col")
        mixed = call(mirror_kernel, shape((row_count, 2 * flat[0], LANES), bf16), parts)(
            tiles, row_pick, row_half, col_half, col_drop, spread, row_rates, pushed
        )
        got = exchange(mixed, "row")
        direct = call(direct_kernel, shape((col_count,) + flat, bf16), parts)(
            tiles, col_pick, col_half, row_half, row_drop, gather, got
        )
        direct = exchange(direct, "col")
        outs = [shape(flat, f32)] * 3
        if step_index < STEPS - 1:
            outs.append(shape((col_count,) + flat, bf16))
        result = call(later_kernel if step_index else first_kernel, tuple(outs))(
            direct, got, rate_log, state, stress, *more
        )
        rate_log, state, stress = result[:3]
        pushed = result[-1]
    return tuple(a.reshape(patches) for a in (rate_log, state, stress))


def solution(mesh):
    in_specs = (P(("row", "col")),) * 9 + (
        P("row", "col", None, None),
        P("row", "col", None, None),
        P("row", "col"),
    )
    out_specs = (P(("row", "col")), P(("row", "col")), P(("row", "col")))
    return jax.shard_map(
        on_device, mesh=mesh, in_specs=in_specs, out_specs=out_specs, check_vma=False
    )
```

```python
import jax
import jax.numpy as jnp
from jax import lax
from jax.experimental import pallas as pl
from jax.experimental.pallas import tpu as pltpu
from jax.sharding import PartitionSpec as P

STEPS = 2
NEWTON = 4
TILE = 64
LANES = 128
WIDTH = 256
ROWS = 128

time_step = 0.25
bf16 = jnp.bfloat16
f32 = jnp.float32


def friction_solve(rate_log, stress, state, normal_stress, rate_param, damping):
    strength = normal_stress * rate_param
    lift = state / rate_param
    for turn_index in range(NEWTON):
        speed = jnp.exp(rate_log)
        ratio = 0.5 * jnp.exp(rate_log + lift)
        root = jnp.sqrt(1.0 + ratio * ratio)
        misfit = stress - damping * speed - strength * jnp.log(ratio + root)
        slope = -damping * speed - strength * ratio / root
        rate_log = rate_log - misfit / slope
    return rate_log


def as_column(row):
    wide = jnp.broadcast_to(row.astype(f32), (LANES, row.shape[1]))
    return jnp.transpose(wide).astype(jnp.int32)


def push_kernel(log_rate_far, places_far, counts, pushed_out, index_out, log_rate, places, sems):
    copies = [
        pltpu.make_async_copy(log_rate_far, log_rate, sems.at[0]),
        pltpu.make_async_copy(places_far, places, sems.at[1]),
    ]
    for copy in copies:
        copy.start()
    for copy in copies:
        copy.wait()
    pushed = (jnp.exp(log_rate[...]) - 1.0).astype(bf16)
    pushed_out[...] = jnp.broadcast_to(pushed[None], pushed_out.shape)
    segment = log_rate.size // TILE
    row_slot, col_slot = places[0:1, :], places[1:2, :]
    live = lax.broadcasted_iota(jnp.int32, row_slot.shape, 1) < counts[0, 0]
    own = col_slot // segment == lax.axis_index("row")
    own = own & (row_slot == lax.axis_index("col") * segment + col_slot % segment)
    index_out[0:1, :] = jnp.where(live, row_slot, -2)
    index_out[1:2, :] = jnp.where(live, col_slot, -2)
    index_out[2:3, :] = jnp.where(live & jnp.logical_not(own), col_slot, -2)


def lower_half(column):
    lane = lax.broadcasted_iota(jnp.int32, column.shape, 1)
    return (lane < TILE) == ((column & 1) == 0)


def chosen(column, rates):
    lane = lax.broadcasted_iota(jnp.int32, column.shape, 1)
    pair = column >> 1
    pick = [
        jnp.where(pair == lane + start, 1.0, 0.0).astype(bf16)
        for start in range(0, rates.shape[0], LANES)
    ]
    both = jnp.dot(jnp.concatenate(pick, axis=1), rates, preferred_element_type=f32)
    return jnp.where(lower_half(column), both, pltpu.roll(both, TILE, 1)).astype(bf16)


def dropped(index, parts, rows):
    tall = lax.broadcasted_iota(jnp.int32, (rows, index.shape[1]), 0)
    drop = jnp.where(tall == (index >> 1), 1.0, 0.0).astype(bf16)
    return jnp.dot(drop, parts, preferred_element_type=f32).astype(bf16)


def fetch(tiles_far, tiles, sems):
    copies = []
    for turn, base in enumerate(range(0, tiles.shape[0], ROWS)):
        rows = pl.ds(base, ROWS)
        copies.append(pltpu.make_async_copy(tiles_far.at[rows, :], tiles.at[rows, :], sems.at[turn]))
        copies[-1].start()
    return copies


def mirror_kernel(tiles, index, rates, pushed, out, spread, parts, *near):
    copies = []
    if near:
        copies = fetch(tiles, *near)
        tiles = near[0]
    entry = lax.broadcasted_iota(jnp.int32, spread.shape, 1) // TILE
    spread[...] = jnp.where(
        entry == lax.broadcasted_iota(jnp.int32, spread.shape, 0), 1.0, 0.0
    ).astype(bf16)
    rates = rates[...].reshape(-1, LANES)
    row_index = index[0:1, :]
    col_index = index[1:2, :]
    for base in range(0, tiles.shape[0], ROWS):
        rows = slice(base, base + ROWS)
        piece = chosen(as_column(row_index[:, rows]), rates)
        if copies:
            copies[base // ROWS].wait()
        total = jnp.zeros((ROWS, LANES), f32)
        for start in range(0, tiles.shape[1], WIDTH):
            wide = jnp.dot(piece, spread[:, start : start + WIDTH], preferred_element_type=f32)
            product = tiles[rows, start : start + WIDTH].astype(f32) * wide
            total += product[:, :LANES] + product[:, LANES:]
        total = total + pltpu.roll(total, TILE, 1)
        half = lower_half(as_column(col_index[:, rows]))
        parts[rows, :] = jnp.where(half, total, 0.0).astype(bf16)
    patches = pushed.shape[1]
    sums = dropped(index[2:3, :], parts[...], pushed.shape[0] * patches)
    out[:, :patches, :] = sums.reshape(pushed.shape)
    out[:, patches:, :] = pushed[...]


def direct_kernel(tiles, index, got, out, gather, parts):
    entry = lax.broadcasted_iota(jnp.int32, gather.shape, 0) // TILE
    gather[...] = jnp.where(
        entry == lax.broadcasted_iota(jnp.int32, gather.shape, 1) % TILE, 1.0, 0.0
    ).astype(bf16)
    patches = out.shape[1]
    rates = got[:, patches:, :].reshape(-1, LANES)
    row_index = index[0:1, :]
    col_index = index[1:2, :]
    for base in range(0, tiles.shape[0], ROWS):
        rows = slice(base, base + ROWS)
        piece = chosen(as_column(col_index[:, rows]), rates)
        piece = jnp.concatenate([piece] * (WIDTH // LANES), axis=1)
        total = jnp.zeros((ROWS, LANES), f32)
        for start in range(0, tiles.shape[1], WIDTH):
            total += jnp.dot(
                tiles[rows, start : start + WIDTH] * piece,
                gather[start : start + WIDTH, :],
                preferred_element_type=f32,
            )
        half = lower_half(as_column(row_index[:, rows]))
        parts[rows, :] = jnp.where(half, total, 0.0).astype(bf16)
    sums = dropped(row_index, parts[...], out.shape[0] * patches)
    out[...] = sums.reshape(out.shape)


def step_body(stress, direct, got, rate_log, state, more, outs):
    normal_stress, rate_param, state_param, slip_length, self_stiffness, damping = (m[...] for m in more)
    rate_out, state_out, stress_out, *pushed_out = outs
    stress_rate = jnp.sum(direct[...].astype(f32), axis=0) + jnp.sum(
        got[:, : direct.shape[1], :].astype(f32), axis=0
    )
    speed = jnp.exp(rate_log)
    new_stress = stress + time_step * (stress_rate - self_stiffness * (speed - 1.0))
    new_state = state + time_step * (state_param / slip_length) * (jnp.exp(-state / state_param) - speed)
    new_rate = friction_solve(rate_log, new_stress, new_state, normal_stress, rate_param, damping)
    rate_out[...] = new_rate
    state_out[...] = new_state
    stress_out[...] = new_stress
    for out in pushed_out:
        pushed = (jnp.exp(new_rate) - 1.0).astype(bf16)
        out[...] = jnp.broadcast_to(pushed[None], out.shape)


def first_kernel(direct, got, log_rate, state, excess, *refs):
    more, outs = refs[:6], refs[6:]
    normal_stress, rate_param, damping = more[0][...], more[1][...], more[5][...]
    rate_log, begin = log_rate[...], state[...]
    ratio = 0.5 * jnp.exp(rate_log + begin / rate_param)
    balance = normal_stress * rate_param * jnp.log(ratio + jnp.sqrt(1.0 + ratio * ratio)) + damping * jnp.exp(
        rate_log
    )
    step_body(balance * (1.0 + excess[...]), direct, got, rate_log, begin, more, outs)


def later_kernel(direct, got, rate_log, state, stress, *refs):
    step_body(stress[...], direct, got, rate_log[...], state[...], refs[:6], refs[6:])


def call(kernel, out_shape, scratch=(), **kw):
    return pl.pallas_call(
        kernel,
        out_shape=out_shape,
        scratch_shapes=list(scratch),
        compiler_params=pltpu.CompilerParams(vmem_limit_bytes=24 << 20),
        **kw,
    )


def on_device(
    log_rate,
    state,
    excess,
    normal_stress,
    rate_param,
    state_param,
    slip_length,
    self_stiffness,
    damping,
    blocks,
    pattern,
    counts,
):
    patches = log_rate.shape[0]
    flat = (patches // LANES, LANES)
    row_count = lax.axis_size("row")
    col_count = lax.axis_size("col")
    slots, tile_size = blocks.shape[2:]
    shape = jax.ShapeDtypeStruct

    tiles = blocks.reshape(slots, tile_size)
    places = pattern.reshape(slots, 2).T
    more = [
        a.reshape(flat)
        for a in (normal_stress, rate_param, state_param, slip_length, self_stiffness, damping)
    ]
    rate_log = log_rate.reshape(flat)
    state = state.reshape(flat)
    stress = excess.reshape(flat)
    vmem = pl.BlockSpec(memory_space=pltpu.VMEM)
    hbm = pl.BlockSpec(memory_space=pltpu.HBM)

    def far(x):
        return pltpu.with_memory_space_constraint(x, pltpu.HBM)

    def exchange(x, axis):
        return lax.all_to_all(x, axis, split_axis=0, concat_axis=0, tiled=True)

    pushed, index = call(
        push_kernel,
        (shape((col_count,) + flat, bf16), shape((8, slots), jnp.int32)),
        (pltpu.VMEM(flat, f32), pltpu.VMEM((2, slots), jnp.int32), pltpu.SemaphoreType.DMA((2,))),
        in_specs=[hbm, hbm, pl.BlockSpec(memory_space=pltpu.SMEM)],
    )(far(rate_log), far(places), counts)
    parts = pltpu.VMEM((slots, LANES), bf16)
    for step_index in range(STEPS):
        row_rates = exchange(pushed, "col")
        near = [pltpu.VMEM((slots, tile_size), bf16), pltpu.SemaphoreType.DMA((slots // ROWS,))]
        mixed = call(
            mirror_kernel,
            shape((row_count, 2 * flat[0], LANES), bf16),
            [pltpu.VMEM((LANES, tile_size), bf16), parts] + ([] if step_index else near),
            in_specs=[vmem if step_index else hbm, vmem, vmem, vmem],
        )(tiles if step_index else far(tiles), index, row_rates, pushed)
        got = exchange(mixed, "row")
        direct = call(
            direct_kernel,
            shape((col_count,) + flat, bf16),
            (pltpu.VMEM((tile_size, LANES), bf16), parts),
        )(tiles, index, got)
        direct = exchange(direct, "col")
        outs = [shape(flat, f32)] * 3
        if step_index < STEPS - 1:
            outs.append(shape((col_count,) + flat, bf16))
        result = call(later_kernel if step_index else first_kernel, tuple(outs))(
            direct, got, rate_log, state, stress, *more
        )
        rate_log, state, stress = result[:3]
        pushed = result[-1]
    return tuple(a.reshape(patches) for a in (rate_log, state, stress))


def solution(mesh):
    in_specs = (P(("row", "col")),) * 9 + (
        P("row", "col", None, None),
        P("row", "col", None, None),
        P("row", "col"),
    )
    out_specs = (P(("row", "col")), P(("row", "col")), P(("row", "col")))
    return jax.shard_map(
        on_device, mesh=mesh, in_specs=in_specs, out_specs=out_specs, check_vma=False
    )
```

```python
import functools

import jax
import jax.numpy as jnp
from jax import lax
from jax.experimental import pallas as pl
from jax.experimental.pallas import tpu as pltpu
from jax.sharding import PartitionSpec as P

STEPS = 2
NEWTON = 4
TILE = 64
LANES = 128
WIDTH = 256
SPAN = 512

time_step = 0.25
bf16 = jnp.bfloat16
f32 = jnp.float32


def friction_solve(rate_log, stress, state, normal_stress, rate_param, damping):
    strength = normal_stress * rate_param
    lift = state / rate_param
    for turn_index in range(NEWTON):
        speed = jnp.exp(rate_log)
        ratio = 0.5 * jnp.exp(rate_log + lift)
        root = jnp.sqrt(1.0 + ratio * ratio)
        misfit = stress - damping * speed - strength * jnp.log(ratio + root)
        slope = -damping * speed - strength * ratio / root
        rate_log = rate_log - misfit / slope
    return rate_log


def push_kernel(log_rate, pushed_out):
    pushed = (jnp.exp(log_rate[...]) - 1.0).astype(bf16)
    pushed_out[...] = jnp.broadcast_to(pushed[None], pushed_out.shape)


def turn_kernel(segment, tiles_far, places_far, counts, turned, index_out, tiles, sems, places, place_sem):
    place_copy = pltpu.make_async_copy(places_far, places, place_sem)
    place_copy.start()
    copies = fetch(tiles_far, tiles, sems, 0)
    place_copy.wait()
    row_slot, col_slot = places[0:1, :], places[1:2, :]
    live = lax.broadcasted_iota(jnp.int32, row_slot.shape, 1) < counts[0, 0]
    own = col_slot // segment == lax.axis_index("row")
    own = own & (row_slot == lax.axis_index("col") * segment + col_slot % segment)
    index_out[0:1, :] = jnp.where(live, row_slot, -2)
    index_out[1:2, :] = jnp.where(live, col_slot, -2)
    index_out[2:3, :] = jnp.where(live & jnp.logical_not(own), col_slot, -2)
    for turn, copy in enumerate(copies):
        copy.wait()
        lanes = slice(turn * SPAN, turn * SPAN + SPAN)
        turned[lanes, :] = jnp.transpose(tiles[:, lanes])


def fetch(tiles_far, tiles, sems, begin):
    copies = []
    for turn, start in enumerate(range(0, tiles.shape[1], SPAN)):
        copies.append(
            pltpu.make_async_copy(
                tiles_far.at[:, pl.ds(begin + start, SPAN)],
                tiles.at[:, pl.ds(start, SPAN)],
                sems.at[turn],
            )
        )
        copies[-1].start()
    return copies


def one_hot(index, rows):
    tall = lax.broadcasted_iota(jnp.int32, (rows, index.shape[1]), 0)
    return jnp.where(tall == (index >> 1), 1.0, 0.0).astype(bf16)


def chosen(index, rates):
    rates = rates.reshape(-1, LANES)
    both = lax.dot_general(
        rates,
        one_hot(index, rates.shape[0]),
        (((0,), (0,)), ((), ())),
        preferred_element_type=f32,
    )
    return jnp.where((index & 1) == 0, both[:TILE, :], both[TILE:, :])


def dropped(index, sums, rows):
    even = (index & 1) == 0
    halves = jnp.concatenate([jnp.where(even, sums, 0.0), jnp.where(even, 0.0, sums)], axis=0)
    return dot_nt(one_hot(index, rows), halves.astype(bf16)).astype(bf16)


def dot_nt(left, right):
    return lax.dot_general(left, right, (((1,), (1,)), ((), ())), preferred_element_type=f32)


def mirror_sums(columns, index, rates, total):
    rate = total.at[1]
    rate[...] = chosen(index, rates)
    fold = lax.broadcasted_iota(jnp.int32, (TILE, WIDTH), 1) % TILE
    fold = jnp.where(fold == lax.broadcasted_iota(jnp.int32, (TILE, WIDTH), 0), 1.0, 0.0).astype(bf16)
    sums = jnp.zeros((TILE, index.shape[1]), f32)
    for first in range(0, TILE, WIDTH // TILE):
        product = []
        for i in range(first, first + WIDTH // TILE):
            wide = jnp.broadcast_to(rate[i : i + 1, :], sums.shape).astype(bf16)
            product.append(columns(i) * wide)
        sums += jnp.dot(fold, jnp.concatenate(product, axis=0), preferred_element_type=f32)
    return sums


def finish_mirror(sums, index, pushed, out):
    patches = pushed.shape[1]
    total = dropped(index[2:3, :], sums, pushed.shape[0] * patches)
    out[:, :patches, :] = total.reshape(pushed.shape)
    out[:, patches:, :] = pushed[...]


def first_mirror_kernel(tiles_far, early, index, rates, pushed, out, late, tiles, total, sems):
    begin = early.shape[0]
    copies = fetch(tiles_far, tiles, sems, begin)
    held = []

    def columns(i):
        start = i * TILE
        if start < begin:
            return early[start : start + TILE, :]
        start -= begin
        if start % SPAN == 0:
            copies[start // SPAN].wait()
            held[:] = [jnp.transpose(tiles[:, start : start + SPAN])]
            late[start : start + SPAN, :] = held[0]
        return held[0][start % SPAN : start % SPAN + TILE, :]

    finish_mirror(mirror_sums(columns, index[0:1, :], rates[...], total), index, pushed, out)


def later_mirror_kernel(early, late, index, rates, pushed, out, total):
    def columns(i):
        start = i * TILE
        if start < early.shape[0]:
            return early[start : start + TILE, :]
        start -= early.shape[0]
        return late[start : start + TILE, :]

    finish_mirror(mirror_sums(columns, index[0:1, :], rates[...], total), index, pushed, out)


def direct_kernel(early, late, index, got, out):
    patches = out.shape[1]
    rate = chosen(index[1:2, :], got[:, patches:, :]).astype(bf16)
    add = lax.broadcasted_iota(jnp.int32, (8, SPAN), 1) // TILE
    add = jnp.where(add == lax.broadcasted_iota(jnp.int32, (8, SPAN), 0), 1.0, 0.0).astype(bf16)
    rate = jnp.concatenate([rate] * (SPAN // TILE), axis=0)
    sums = [
        jnp.dot(add, turned[start : start + SPAN, :] * rate, preferred_element_type=f32)
        for turned in (early, late)
        for start in range(0, turned.shape[0], SPAN)
    ]
    sums = jnp.concatenate(sums, axis=0)
    out[...] = dropped(index[0:1, :], sums, out.shape[0] * patches).reshape(out.shape)


def step_body(stress, direct, got, rate_log, state, more, outs):
    normal_stress, rate_param, state_param, slip_length, self_stiffness, damping = (m[...] for m in more)
    rate_out, state_out, stress_out, *pushed_out = outs
    stress_rate = jnp.sum(direct[...].astype(f32), axis=0) + jnp.sum(
        got[:, : direct.shape[1], :].astype(f32), axis=0
    )
    speed = jnp.exp(rate_log)
    new_stress = stress + time_step * (stress_rate - self_stiffness * (speed - 1.0))
    new_state = state + time_step * (state_param / slip_length) * (jnp.exp(-state / state_param) - speed)
    new_rate = friction_solve(rate_log, new_stress, new_state, normal_stress, rate_param, damping)
    rate_out[...] = new_rate
    state_out[...] = new_state
    stress_out[...] = new_stress
    for out in pushed_out:
        pushed = (jnp.exp(new_rate) - 1.0).astype(bf16)
        out[...] = jnp.broadcast_to(pushed[None], out.shape)


def first_kernel(direct, got, log_rate, state, excess, *refs):
    more, outs = refs[:6], refs[6:]
    normal_stress, rate_param, damping = more[0][...], more[1][...], more[5][...]
    rate_log, begin = log_rate[...], state[...]
    ratio = 0.5 * jnp.exp(rate_log + begin / rate_param)
    balance = normal_stress * rate_param * jnp.log(ratio + jnp.sqrt(1.0 + ratio * ratio)) + damping * jnp.exp(
        rate_log
    )
    step_body(balance * (1.0 + excess[...]), direct, got, rate_log, begin, more, outs)


def later_kernel(direct, got, rate_log, state, stress, *refs):
    step_body(stress[...], direct, got, rate_log[...], state[...], refs[:6], refs[6:])


def call(kernel, out_shape, scratch=(), **kw):
    return pl.pallas_call(
        kernel,
        out_shape=out_shape,
        scratch_shapes=list(scratch),
        compiler_params=pltpu.CompilerParams(vmem_limit_bytes=24 << 20),
        **kw,
    )


def on_device(
    log_rate,
    state,
    excess,
    normal_stress,
    rate_param,
    state_param,
    slip_length,
    self_stiffness,
    damping,
    blocks,
    pattern,
    counts,
):
    patches = log_rate.shape[0]
    flat = (patches // LANES, LANES)
    row_count = lax.axis_size("row")
    col_count = lax.axis_size("col")
    slots, tile_size = blocks.shape[2:]
    shape = jax.ShapeDtypeStruct

    tiles = blocks.reshape(slots, tile_size)
    places = pattern.reshape(slots, 2).T
    more = [
        a.reshape(flat)
        for a in (normal_stress, rate_param, state_param, slip_length, self_stiffness, damping)
    ]
    rate_log = log_rate.reshape(flat)
    state = state.reshape(flat)
    stress = excess.reshape(flat)
    vmem = pl.BlockSpec(memory_space=pltpu.VMEM)
    hbm = pl.BlockSpec(memory_space=pltpu.HBM)

    def far(x):
        return pltpu.with_memory_space_constraint(x, pltpu.HBM)

    def exchange(x, axis):
        return lax.all_to_all(x, axis, split_axis=0, concat_axis=0, tiled=True)

    pushed = call(push_kernel, shape((col_count,) + flat, bf16), )(far(rate_log))
    half = tile_size // 2
    landing = (
        pltpu.VMEM((slots, half), bf16),
        pltpu.SemaphoreType.DMA((half // SPAN,)),
    )
    turned = (shape((half, slots), bf16),)
    early, index = call(
        functools.partial(turn_kernel, patches // TILE),
        turned + (shape((8, slots), jnp.int32),),
        landing + (pltpu.VMEM((2, slots), jnp.int32), pltpu.SemaphoreType.DMA),
        in_specs=[hbm, hbm, pl.BlockSpec(memory_space=pltpu.SMEM)],
    )(far(tiles), far(places), counts)
    total = pltpu.VMEM((2, TILE, slots), f32)
    mixed_shape = shape((row_count, 2 * flat[0], LANES), bf16)
    for step_index in range(STEPS):
        row_rates = exchange(pushed, "col")
        if step_index:
            mixed = call(later_mirror_kernel, mixed_shape, (total,))(early, late, index, row_rates, pushed)
        else:
            mixed, late = call(
                first_mirror_kernel,
                (mixed_shape,) + turned,
                (landing[0], total, landing[1]),
                in_specs=[hbm, vmem, vmem, vmem, vmem],
            )(far(tiles), early, index, row_rates, pushed)
        got = exchange(mixed, "row")
        direct = call(direct_kernel, shape((col_count,) + flat, bf16))(early, late, index, got)
        direct = exchange(direct, "col")
        outs = [shape(flat, f32)] * 3
        if step_index < STEPS - 1:
            outs.append(shape((col_count,) + flat, bf16))
        result = call(later_kernel if step_index else first_kernel, tuple(outs))(
            direct, got, rate_log, state, stress, *more
        )
        rate_log, state, stress = result[:3]
        pushed = result[-1]
    return tuple(a.reshape(patches) for a in (rate_log, state, stress))


def solution(mesh):
    in_specs = (P(("row", "col")),) * 9 + (
        P("row", "col", None, None),
        P("row", "col", None, None),
        P("row", "col"),
    )
    out_specs = (P(("row", "col")), P(("row", "col")), P(("row", "col")))
    return jax.shard_map(
        on_device, mesh=mesh, in_specs=in_specs, out_specs=out_specs, check_vma=False
    )
```

```python
import functools

import jax
import jax.numpy as jnp
from jax import lax
from jax.experimental import pallas as pl
from jax.experimental.pallas import tpu as pltpu
from jax.sharding import PartitionSpec as P

STEPS = 2
NEWTON = 4
TILE = 64
LANES = 128
WIDTH = 256
SPAN = 512

ORDER = {"row": 12, "col": 13}

time_step = 0.25
bf16 = jnp.bfloat16
f32 = jnp.float32


def friction_solve(rate_log, stress, state, normal_stress, rate_param, damping):
    strength = normal_stress * rate_param
    lift = state / rate_param
    for turn_index in range(NEWTON):
        speed = jnp.exp(rate_log)
        ratio = 0.5 * jnp.exp(rate_log + lift)
        root = jnp.sqrt(1.0 + ratio * ratio)
        misfit = stress - damping * speed - strength * jnp.log(ratio + root)
        slope = -damping * speed - strength * ratio / root
        rate_log = rate_log - misfit / slope
    return rate_log


def push_kernel(log_rate, pushed_out):
    pushed = (jnp.exp(log_rate[...]) - 1.0).astype(bf16)
    pushed_out[...] = jnp.broadcast_to(pushed[None], pushed_out.shape)


def turn_kernel(segment, tiles_far, places_far, counts, turned, index_out, tiles, sems, places, place_sem):
    place_copy = pltpu.make_async_copy(places_far, places, place_sem)
    place_copy.start()
    copies = fetch(tiles_far, tiles, sems, 0)
    place_copy.wait()
    row_slot, col_slot = places[0:1, :], places[1:2, :]
    live = lax.broadcasted_iota(jnp.int32, row_slot.shape, 1) < counts[0, 0]
    own = col_slot // segment == lax.axis_index("row")
    own = own & (row_slot == lax.axis_index("col") * segment + col_slot % segment)
    row_slot = row_slot ^ (segment * ORDER["col"])
    col_slot = col_slot ^ (segment * ORDER["row"])
    index_out[0:1, :] = jnp.where(live, row_slot, -2)
    index_out[1:2, :] = jnp.where(live, col_slot, -2)
    index_out[2:3, :] = jnp.where(live & jnp.logical_not(own), col_slot, -2)
    for turn, copy in enumerate(copies):
        copy.wait()
        lanes = slice(turn * SPAN, turn * SPAN + SPAN)
        turned[lanes, :] = jnp.transpose(tiles[:, lanes])


def fetch(tiles_far, tiles, sems, begin):
    copies = []
    for turn, start in enumerate(range(0, tiles.shape[1], SPAN)):
        copies.append(
            pltpu.make_async_copy(
                tiles_far.at[:, pl.ds(begin + start, SPAN)],
                tiles.at[:, pl.ds(start, SPAN)],
                sems.at[turn],
            )
        )
        copies[-1].start()
    return copies


def one_hot(index, rows):
    tall = lax.broadcasted_iota(jnp.int32, (rows, index.shape[1]), 0)
    return jnp.where(tall == (index >> 1), 1.0, 0.0).astype(bf16)


def chosen(index, rates):
    rates = rates.reshape(-1, LANES)
    both = lax.dot_general(
        rates,
        one_hot(index, rates.shape[0]),
        (((0,), (0,)), ((), ())),
        preferred_element_type=f32,
    )
    return jnp.where((index & 1) == 0, both[:TILE, :], both[TILE:, :])


def dropped(index, sums, rows):
    even = (index & 1) == 0
    halves = jnp.concatenate([jnp.where(even, sums, 0.0), jnp.where(even, 0.0, sums)], axis=0)
    return dot_nt(one_hot(index, rows), halves.astype(bf16)).astype(bf16)


def dot_nt(left, right):
    return lax.dot_general(left, right, (((1,), (1,)), ((), ())), preferred_element_type=f32)


def mirror_sums(columns, index, rates, total):
    rate = total.at[1]
    rate[...] = chosen(index, rates)
    fold = lax.broadcasted_iota(jnp.int32, (TILE, WIDTH), 1) % TILE
    fold = jnp.where(fold == lax.broadcasted_iota(jnp.int32, (TILE, WIDTH), 0), 1.0, 0.0).astype(bf16)
    sums = jnp.zeros((TILE, index.shape[1]), f32)
    for first in range(0, TILE, WIDTH // TILE):
        product = []
        for i in range(first, first + WIDTH // TILE):
            wide = jnp.broadcast_to(rate[i : i + 1, :], sums.shape).astype(bf16)
            product.append(columns(i) * wide)
        sums += jnp.dot(fold, jnp.concatenate(product, axis=0), preferred_element_type=f32)
    return sums


def finish_mirror(sums, index, rates, out):
    groups, patches = rates.shape[:2]
    total = dropped(index[2:3, :], sums, groups * patches)
    out[:, :patches, :] = total.reshape(rates.shape)
    own = rates[pl.ds(lax.axis_index("col") ^ ORDER["col"], 1), :, :]
    out[:, patches:, :] = jnp.broadcast_to(own, rates.shape)


def first_mirror_kernel(tiles_far, early, index, rates, out, late, total, tiles, sems):
    begin = early.shape[0]
    copies = fetch(tiles_far, tiles, sems, begin)
    held = []

    def columns(i):
        start = i * TILE
        if start < begin:
            return early[start : start + TILE, :]
        start -= begin
        if start % SPAN == 0:
            copies[start // SPAN].wait()
            held[:] = [jnp.transpose(tiles[:, start : start + SPAN])]
            late[start : start + SPAN, :] = held[0]
        return held[0][start % SPAN : start % SPAN + TILE, :]

    finish_mirror(mirror_sums(columns, index[0:1, :], rates[...], total), index, rates, out)


def later_mirror_kernel(early, late, index, rates, out, total):
    def columns(i):
        start = i * TILE
        if start < early.shape[0]:
            return early[start : start + TILE, :]
        start -= early.shape[0]
        return late[start : start + TILE, :]

    finish_mirror(mirror_sums(columns, index[0:1, :], rates[...], total), index, rates, out)


def direct_kernel(early, late, index, got, out):
    patches = out.shape[1]
    rate = chosen(index[1:2, :], got[:, patches:, :]).astype(bf16)
    add = lax.broadcasted_iota(jnp.int32, (8, SPAN), 1) // TILE
    add = jnp.where(add == lax.broadcasted_iota(jnp.int32, (8, SPAN), 0), 1.0, 0.0).astype(bf16)
    rate = jnp.concatenate([rate] * (SPAN // TILE), axis=0)
    sums = [
        jnp.dot(add, turned[start : start + SPAN, :] * rate, preferred_element_type=f32)
        for turned in (early, late)
        for start in range(0, turned.shape[0], SPAN)
    ]
    sums = jnp.concatenate(sums, axis=0)
    out[...] = dropped(index[0:1, :], sums, out.shape[0] * patches).reshape(out.shape)


def step_body(stress, direct, got, rate_log, state, more, outs):
    normal_stress, rate_param, state_param, slip_length, self_stiffness, damping = (m[...] for m in more)
    rate_out, state_out, stress_out, *pushed_out = outs
    stress_rate = jnp.sum(direct[...].astype(f32), axis=0) + jnp.sum(
        got[:, : direct.shape[1], :].astype(f32), axis=0
    )
    speed = jnp.exp(rate_log)
    new_stress = stress + time_step * (stress_rate - self_stiffness * (speed - 1.0))
    new_state = state + time_step * (state_param / slip_length) * (jnp.exp(-state / state_param) - speed)
    new_rate = friction_solve(rate_log, new_stress, new_state, normal_stress, rate_param, damping)
    rate_out[...] = new_rate
    state_out[...] = new_state
    stress_out[...] = new_stress
    for out in pushed_out:
        pushed = (jnp.exp(new_rate) - 1.0).astype(bf16)
        out[...] = jnp.broadcast_to(pushed[None], out.shape)


def first_kernel(direct, got, log_rate, state, excess, *refs):
    more, outs = refs[:6], refs[6:]
    normal_stress, rate_param, damping = more[0][...], more[1][...], more[5][...]
    rate_log, begin = log_rate[...], state[...]
    ratio = 0.5 * jnp.exp(rate_log + begin / rate_param)
    balance = normal_stress * rate_param * jnp.log(ratio + jnp.sqrt(1.0 + ratio * ratio)) + damping * jnp.exp(
        rate_log
    )
    step_body(balance * (1.0 + excess[...]), direct, got, rate_log, begin, more, outs)


def later_kernel(direct, got, rate_log, state, stress, *refs):
    step_body(stress[...], direct, got, rate_log[...], state[...], refs[:6], refs[6:])


def call(kernel, out_shape, scratch=(), **kw):
    return pl.pallas_call(
        kernel,
        out_shape=out_shape,
        scratch_shapes=list(scratch),
        compiler_params=pltpu.CompilerParams(vmem_limit_bytes=24 << 20),
        **kw,
    )


def on_device(
    log_rate,
    state,
    excess,
    normal_stress,
    rate_param,
    state_param,
    slip_length,
    self_stiffness,
    damping,
    blocks,
    pattern,
    counts,
):
    patches = log_rate.shape[0]
    flat = (patches // LANES, LANES)
    row_count = lax.axis_size("row")
    col_count = lax.axis_size("col")
    slots, tile_size = blocks.shape[2:]
    shape = jax.ShapeDtypeStruct

    tiles = blocks.reshape(slots, tile_size)
    places = pattern.reshape(slots, 2).T
    more = [
        a.reshape(flat)
        for a in (normal_stress, rate_param, state_param, slip_length, self_stiffness, damping)
    ]
    rate_log = log_rate.reshape(flat)
    state = state.reshape(flat)
    stress = excess.reshape(flat)
    vmem = pl.BlockSpec(memory_space=pltpu.VMEM)
    hbm = pl.BlockSpec(memory_space=pltpu.HBM)

    def far(x):
        return pltpu.with_memory_space_constraint(x, pltpu.HBM)

    def exchange(x, axis):
        order = [k ^ ORDER[axis] for k in range(x.shape[0])]
        return lax.all_to_all(
            x, axis, split_axis=0, concat_axis=0, tiled=True, axis_index_groups=[order]
        )

    pushed = call(push_kernel, shape((col_count,) + flat, bf16), )(far(rate_log))
    begin = tile_size // 4 * 3

    def landing(lanes):
        return (pltpu.VMEM((slots, lanes), bf16), pltpu.SemaphoreType.DMA((lanes // SPAN,)))

    early, index = call(
        functools.partial(turn_kernel, patches // TILE),
        (shape((begin, slots), bf16), shape((8, slots), jnp.int32)),
        landing(begin) + (pltpu.VMEM((2, slots), jnp.int32), pltpu.SemaphoreType.DMA),
        in_specs=[hbm, hbm, pl.BlockSpec(memory_space=pltpu.SMEM)],
    )(far(tiles), far(places), counts)
    total = pltpu.VMEM((2, TILE, slots), f32)
    mixed_shape = shape((row_count, 2 * flat[0], LANES), bf16)
    for step_index in range(STEPS):
        row_rates = exchange(pushed, "col")
        if step_index:
            mixed = call(later_mirror_kernel, mixed_shape, (total,))(early, late, index, row_rates)
        else:
            mixed, late = call(
                first_mirror_kernel,
                (mixed_shape, shape((tile_size - begin, slots), bf16)),
                (total,) + landing(tile_size - begin),
                in_specs=[hbm, vmem, vmem, vmem],
            )(far(tiles), early, index, row_rates)
        got = exchange(mixed, "row")
        direct = call(direct_kernel, shape((col_count,) + flat, bf16))(early, late, index, got)
        direct = exchange(direct, "col")
        outs = [shape(flat, f32)] * 3
        if step_index < STEPS - 1:
            outs.append(shape((col_count,) + flat, bf16))
        result = call(later_kernel if step_index else first_kernel, tuple(outs))(
            direct, got, rate_log, state, stress, *more
        )
        rate_log, state, stress = result[:3]
        pushed = result[-1]
    return tuple(a.reshape(patches) for a in (rate_log, state, stress))


def solution(mesh):
    in_specs = (P(("row", "col")),) * 9 + (
        P("row", "col", None, None),
        P("row", "col", None, None),
        P("row", "col"),
    )
    out_specs = (P(("row", "col")), P(("row", "col")), P(("row", "col")))
    return jax.shard_map(
        on_device, mesh=mesh, in_specs=in_specs, out_specs=out_specs, check_vma=False
    )
```

```python
import functools

import jax
import jax.numpy as jnp
from jax import lax
from jax.experimental import pallas as pl
from jax.experimental.pallas import tpu as pltpu
from jax.sharding import PartitionSpec as P

STEPS = 2
NEWTON = 4
TILE = 64
LANES = 128
WIDTH = 256
SPAN = 512

ORDER = {"row": 12, "col": 13}

time_step = 0.25
bf16 = jnp.bfloat16
f32 = jnp.float32


def friction_solve(rate_log, stress, state, normal_stress, rate_param, damping):
    strength = normal_stress * rate_param
    lift = state / rate_param
    for turn_index in range(NEWTON):
        speed = jnp.exp(rate_log)
        ratio = 0.5 * jnp.exp(rate_log + lift)
        root = jnp.sqrt(1.0 + ratio * ratio)
        misfit = stress - damping * speed - strength * jnp.log(ratio + root)
        slope = -damping * speed - strength * ratio / root
        rate_log = rate_log - misfit / slope
    return rate_log


def push_kernel(log_rate, pushed_out):
    pushed = (jnp.exp(log_rate[...]) - 1.0).astype(bf16)
    pushed_out[...] = jnp.broadcast_to(pushed[None], pushed_out.shape)


def turn_kernel(segment, tiles_far, places_far, counts, turned, index_out, tiles, sems, places, place_sem):
    place_copy = pltpu.make_async_copy(places_far, places, place_sem)
    place_copy.start()
    copies = []
    for turn, base in enumerate(range(0, tiles.shape[0], LANES)):
        rows = pl.ds(base, LANES)
        far = tiles_far.at[rows, pl.ds(0, tiles.shape[1])]
        copies.append(pltpu.make_async_copy(far, tiles.at[rows, :], sems.at[turn]))
        copies[-1].start()
    place_copy.wait()
    row_slot, col_slot = places[0:1, :], places[1:2, :]
    live = lax.broadcasted_iota(jnp.int32, row_slot.shape, 1) < counts[0, 0]
    own = col_slot // segment == lax.axis_index("row")
    own = own & (row_slot == lax.axis_index("col") * segment + col_slot % segment)
    row_slot = row_slot ^ (segment * ORDER["col"])
    col_slot = col_slot ^ (segment * ORDER["row"])
    index_out[0:1, :] = jnp.where(live, row_slot, -2)
    index_out[1:2, :] = jnp.where(live, col_slot, -2)
    index_out[2:3, :] = jnp.where(live & jnp.logical_not(own), col_slot, -2)
    for turn, copy in enumerate(copies):
        copy.wait()
        rows = slice(turn * LANES, turn * LANES + LANES)
        for start in range(0, tiles.shape[1], SPAN):
            lanes = slice(start, start + SPAN)
            turned[lanes, rows] = jnp.transpose(tiles[rows, lanes])


def fetch(tiles_far, tiles, sems, begin):
    copies = []
    for turn, start in enumerate(range(0, tiles.shape[1], SPAN)):
        copies.append(
            pltpu.make_async_copy(
                tiles_far.at[:, pl.ds(begin + start, SPAN)],
                tiles.at[:, pl.ds(start, SPAN)],
                sems.at[turn],
            )
        )
        copies[-1].start()
    return copies


def one_hot(index, rows):
    tall = lax.broadcasted_iota(jnp.int32, (rows, index.shape[1]), 0)
    return jnp.where(tall == (index >> 1), 1.0, 0.0).astype(bf16)


def chosen(index, rates):
    rates = rates.reshape(-1, LANES)
    both = lax.dot_general(
        rates,
        one_hot(index, rates.shape[0]),
        (((0,), (0,)), ((), ())),
        preferred_element_type=f32,
    )
    return jnp.where((index & 1) == 0, both[:TILE, :], both[TILE:, :])


def dropped(index, sums, rows):
    even = (index & 1) == 0
    halves = jnp.concatenate([jnp.where(even, sums, 0.0), jnp.where(even, 0.0, sums)], axis=0)
    return dot_nt(one_hot(index, rows), halves.astype(bf16)).astype(bf16)


def dot_nt(left, right):
    return lax.dot_general(left, right, (((1,), (1,)), ((), ())), preferred_element_type=f32)


def mirror_sums(columns, index, rates, total):
    rate = total.at[1]
    rate[...] = chosen(index, rates)
    fold = lax.broadcasted_iota(jnp.int32, (TILE, WIDTH), 1) % TILE
    fold = jnp.where(fold == lax.broadcasted_iota(jnp.int32, (TILE, WIDTH), 0), 1.0, 0.0).astype(bf16)
    sums = jnp.zeros((TILE, index.shape[1]), f32)
    for first in range(0, TILE, WIDTH // TILE):
        product = []
        for i in range(first, first + WIDTH // TILE):
            wide = jnp.broadcast_to(rate[i : i + 1, :], sums.shape).astype(bf16)
            product.append(columns(i) * wide)
        sums += jnp.dot(fold, jnp.concatenate(product, axis=0), preferred_element_type=f32)
    return sums


def finish_mirror(sums, index, rates, out):
    groups, patches = rates.shape[:2]
    total = dropped(index[2:3, :], sums, groups * patches)
    out[:, :patches, :] = total.reshape(rates.shape)
    own = rates[pl.ds(lax.axis_index("col") ^ ORDER["col"], 1), :, :]
    out[:, patches:, :] = jnp.broadcast_to(own, rates.shape)


def first_mirror_kernel(tiles_far, early, index, rates, out, late, total, tiles, sems):
    begin = early.shape[0]
    copies = fetch(tiles_far, tiles, sems, begin)
    held = []

    def columns(i):
        start = i * TILE
        if start < begin:
            return early[start : start + TILE, :]
        start -= begin
        if start % SPAN == 0:
            copies[start // SPAN].wait()
            held[:] = [jnp.transpose(tiles[:, start : start + SPAN])]
            late[start : start + SPAN, :] = held[0]
        return held[0][start % SPAN : start % SPAN + TILE, :]

    finish_mirror(mirror_sums(columns, index[0:1, :], rates[...], total), index, rates, out)


def later_mirror_kernel(early, late, index, rates, out, total):
    def columns(i):
        start = i * TILE
        if start < early.shape[0]:
            return early[start : start + TILE, :]
        start -= early.shape[0]
        return late[start : start + TILE, :]

    finish_mirror(mirror_sums(columns, index[0:1, :], rates[...], total), index, rates, out)


def direct_kernel(early, late, index, got, out):
    patches = out.shape[1]
    rate = chosen(index[1:2, :], got[:, patches:, :]).astype(bf16)
    add = lax.broadcasted_iota(jnp.int32, (8, SPAN), 1) // TILE
    add = jnp.where(add == lax.broadcasted_iota(jnp.int32, (8, SPAN), 0), 1.0, 0.0).astype(bf16)
    rate = jnp.concatenate([rate] * (SPAN // TILE), axis=0)
    sums = [
        jnp.dot(add, turned[start : start + SPAN, :] * rate, preferred_element_type=f32)
        for turned in (early, late)
        for start in range(0, turned.shape[0], SPAN)
    ]
    sums = jnp.concatenate(sums, axis=0)
    out[...] = dropped(index[0:1, :], sums, out.shape[0] * patches).reshape(out.shape)


def step_body(stress, direct, got, rate_log, state, more, outs):
    normal_stress, rate_param, state_param, slip_length, self_stiffness, damping = (m[...] for m in more)
    rate_out, state_out, stress_out, *pushed_out = outs
    stress_rate = jnp.sum(direct[...].astype(f32), axis=0) + jnp.sum(
        got[:, : direct.shape[1], :].astype(f32), axis=0
    )
    speed = jnp.exp(rate_log)
    new_stress = stress + time_step * (stress_rate - self_stiffness * (speed - 1.0))
    new_state = state + time_step * (state_param / slip_length) * (jnp.exp(-state / state_param) - speed)
    new_rate = friction_solve(rate_log, new_stress, new_state, normal_stress, rate_param, damping)
    rate_out[...] = new_rate
    state_out[...] = new_state
    stress_out[...] = new_stress
    for out in pushed_out:
        pushed = (jnp.exp(new_rate) - 1.0).astype(bf16)
        out[...] = jnp.broadcast_to(pushed[None], out.shape)


def first_kernel(direct, got, log_rate, state, excess, *refs):
    more, outs = refs[:6], refs[6:]
    normal_stress, rate_param, damping = more[0][...], more[1][...], more[5][...]
    rate_log, begin = log_rate[...], state[...]
    ratio = 0.5 * jnp.exp(rate_log + begin / rate_param)
    balance = normal_stress * rate_param * jnp.log(ratio + jnp.sqrt(1.0 + ratio * ratio)) + damping * jnp.exp(
        rate_log
    )
    step_body(balance * (1.0 + excess[...]), direct, got, rate_log, begin, more, outs)


def later_kernel(direct, got, rate_log, state, stress, *refs):
    step_body(stress[...], direct, got, rate_log[...], state[...], refs[:6], refs[6:])


def call(kernel, out_shape, scratch=(), **kw):
    return pl.pallas_call(
        kernel,
        out_shape=out_shape,
        scratch_shapes=list(scratch),
        compiler_params=pltpu.CompilerParams(vmem_limit_bytes=24 << 20),
        **kw,
    )


def on_device(
    log_rate,
    state,
    excess,
    normal_stress,
    rate_param,
    state_param,
    slip_length,
    self_stiffness,
    damping,
    blocks,
    pattern,
    counts,
):
    patches = log_rate.shape[0]
    flat = (patches // LANES, LANES)
    row_count = lax.axis_size("row")
    col_count = lax.axis_size("col")
    slots, tile_size = blocks.shape[2:]
    shape = jax.ShapeDtypeStruct

    tiles = blocks.reshape(slots, tile_size)
    places = pattern.reshape(slots, 2).T
    more = [
        a.reshape(flat)
        for a in (normal_stress, rate_param, state_param, slip_length, self_stiffness, damping)
    ]
    rate_log = log_rate.reshape(flat)
    state = state.reshape(flat)
    stress = excess.reshape(flat)
    vmem = pl.BlockSpec(memory_space=pltpu.VMEM)
    hbm = pl.BlockSpec(memory_space=pltpu.HBM)

    def far(x):
        return pltpu.with_memory_space_constraint(x, pltpu.HBM)

    def exchange(x, axis):
        order = [k ^ ORDER[axis] for k in range(x.shape[0])]
        return lax.all_to_all(
            x, axis, split_axis=0, concat_axis=0, tiled=True, axis_index_groups=[order]
        )

    pushed = call(push_kernel, shape((col_count,) + flat, bf16), )(far(rate_log))
    begin = tile_size // 4 * 3

    def landing(lanes, copies):
        return (pltpu.VMEM((slots, lanes), bf16), pltpu.SemaphoreType.DMA((copies,)))

    early, index = call(
        functools.partial(turn_kernel, patches // TILE),
        (shape((begin, slots), bf16), shape((8, slots), jnp.int32)),
        landing(begin, slots // LANES) + (pltpu.VMEM((2, slots), jnp.int32), pltpu.SemaphoreType.DMA),
        in_specs=[hbm, hbm, pl.BlockSpec(memory_space=pltpu.SMEM)],
    )(far(tiles), far(places), counts)
    total = pltpu.VMEM((2, TILE, slots), f32)
    mixed_shape = shape((row_count, 2 * flat[0], LANES), bf16)
    for step_index in range(STEPS):
        row_rates = exchange(pushed, "col")
        if step_index:
            mixed = call(later_mirror_kernel, mixed_shape, (total,))(early, late, index, row_rates)
        else:
            mixed, late = call(
                first_mirror_kernel,
                (mixed_shape, shape((tile_size - begin, slots), bf16)),
                (total,) + landing(tile_size - begin, (tile_size - begin) // SPAN),
                in_specs=[hbm, vmem, vmem, vmem],
            )(far(tiles), early, index, row_rates)
        got = exchange(mixed, "row")
        direct = call(direct_kernel, shape((col_count,) + flat, bf16))(early, late, index, got)
        direct = exchange(direct, "col")
        outs = [shape(flat, f32)] * 3
        if step_index < STEPS - 1:
            outs.append(shape((col_count,) + flat, bf16))
        result = call(later_kernel if step_index else first_kernel, tuple(outs))(
            direct, got, rate_log, state, stress, *more
        )
        rate_log, state, stress = result[:3]
        pushed = result[-1]
    return tuple(a.reshape(patches) for a in (rate_log, state, stress))


def solution(mesh):
    in_specs = (P(("row", "col")),) * 9 + (
        P("row", "col", None, None),
        P("row", "col", None, None),
        P("row", "col"),
    )
    out_specs = (P(("row", "col")), P(("row", "col")), P(("row", "col")))
    return jax.shard_map(
        on_device, mesh=mesh, in_specs=in_specs, out_specs=out_specs, check_vma=False
    )
```

```python
import functools

import jax
import jax.numpy as jnp
from jax import lax
from jax.experimental import pallas as pl
from jax.experimental.pallas import tpu as pltpu
from jax.sharding import PartitionSpec as P

STEPS = 2
NEWTON = 4
TILE = 64
LANES = 128
WIDTH = 256
SPAN = 512

ORDER = {"row": 12, "col": 13}

time_step = 0.25
bf16 = jnp.bfloat16
f32 = jnp.float32


def friction_solve(rate_log, stress, state, normal_stress, rate_param, damping):
    strength = normal_stress * rate_param
    lift = state / rate_param
    for turn_index in range(NEWTON):
        speed = jnp.exp(rate_log)
        ratio = 0.5 * jnp.exp(rate_log + lift)
        root = jnp.sqrt(1.0 + ratio * ratio)
        misfit = stress - damping * speed - strength * jnp.log(ratio + root)
        slope = -damping * speed - strength * ratio / root
        rate_log = rate_log - misfit / slope
    return rate_log


def push_kernel(log_rate, pushed_out):
    pushed = (jnp.exp(log_rate[...]) - 1.0).astype(bf16)
    pushed_out[...] = jnp.broadcast_to(pushed[None], pushed_out.shape)


def turn_kernel(segment, tiles_far, places_far, counts, turned, index_out, tiles, sems, places, place_sem):
    place_copy = pltpu.make_async_copy(places_far, places, place_sem)
    place_copy.start()
    copies = []
    for turn, base in enumerate(range(0, tiles.shape[0], LANES)):
        rows = pl.ds(base, LANES)
        far = tiles_far.at[rows, pl.ds(0, tiles.shape[1])]
        copies.append(pltpu.make_async_copy(far, tiles.at[rows, :], sems.at[turn]))
        copies[-1].start()
    place_copy.wait()
    row_slot, col_slot = places[0:1, :], places[1:2, :]
    live = lax.broadcasted_iota(jnp.int32, row_slot.shape, 1) < counts[0, 0]
    own = col_slot // segment == lax.axis_index("row")
    own = own & (row_slot == lax.axis_index("col") * segment + col_slot % segment)
    row_slot = row_slot ^ (segment * ORDER["col"])
    col_slot = col_slot ^ (segment * ORDER["row"])
    index_out[0:1, :] = jnp.where(live, row_slot, -2)
    index_out[1:2, :] = jnp.where(live, col_slot, -2)
    index_out[2:3, :] = jnp.where(live & jnp.logical_not(own), col_slot, -2)
    for turn, copy in enumerate(copies):
        copy.wait()
        rows = slice(turn * LANES, turn * LANES + LANES)
        for start in range(0, tiles.shape[1], SPAN):
            lanes = slice(start, start + SPAN)
            turned[lanes, rows] = jnp.transpose(tiles[rows, lanes])


def fetch(tiles_far, tiles, sems, begin):
    copies = []
    for turn, start in enumerate(range(0, tiles.shape[1], SPAN)):
        copies.append(
            pltpu.make_async_copy(
                tiles_far.at[:, pl.ds(begin + start, SPAN)],
                tiles.at[:, pl.ds(start, SPAN)],
                sems.at[turn],
            )
        )
        copies[-1].start()
    return copies


def one_hot(index, rows):
    tall = lax.broadcasted_iota(jnp.int32, (rows, index.shape[1]), 0)
    return jnp.where(tall == (index >> 1), 1.0, 0.0).astype(bf16)


def chosen(index, rates):
    rates = rates.reshape(-1, LANES)
    both = lax.dot_general(
        rates,
        one_hot(index, rates.shape[0]),
        (((0,), (0,)), ((), ())),
        preferred_element_type=f32,
    )
    return jnp.where((index & 1) == 0, both[:TILE, :], both[TILE:, :])


def dropped(index, sums, rows):
    even = (index & 1) == 0
    halves = jnp.concatenate([jnp.where(even, sums, 0.0), jnp.where(even, 0.0, sums)], axis=0)
    return dot_nt(one_hot(index, rows), halves.astype(bf16)).astype(bf16)


def dot_nt(left, right):
    return lax.dot_general(left, right, (((1,), (1,)), ((), ())), preferred_element_type=f32)


def mirror_sums(columns, index, rates, total):
    rate = total.at[1]
    rate[...] = chosen(index, rates)
    fold = lax.broadcasted_iota(jnp.int32, (TILE, WIDTH), 1) % TILE
    fold = jnp.where(fold == lax.broadcasted_iota(jnp.int32, (TILE, WIDTH), 0), 1.0, 0.0).astype(bf16)
    sums = jnp.zeros((TILE, index.shape[1]), f32)
    for first in range(0, TILE, WIDTH // TILE):
        product = []
        for i in range(first, first + WIDTH // TILE):
            wide = jnp.broadcast_to(rate[i : i + 1, :], sums.shape).astype(bf16)
            product.append(columns(i) * wide)
        sums += jnp.dot(fold, jnp.concatenate(product, axis=0), preferred_element_type=f32)
    return sums


def finish_mirror(sums, index, rates, out):
    groups, patches = rates.shape[:2]
    total = dropped(index[2:3, :], sums, groups * patches)
    out[:, :patches, :] = total.reshape(rates.shape)
    own = rates[pl.ds(lax.axis_index("col") ^ ORDER["col"], 1), :, :]
    out[:, patches:, :] = jnp.broadcast_to(own, rates.shape)


def first_mirror_kernel(tiles_far, early, index, rates, out, late, total, tiles, sems):
    begin = early.shape[0]
    copies = fetch(tiles_far, tiles, sems, begin)
    held = []

    def columns(i):
        start = i * TILE
        if start < begin:
            return early[start : start + TILE, :]
        start -= begin
        if start % SPAN == 0:
            copies[start // SPAN].wait()
            held[:] = [jnp.transpose(tiles[:, start : start + SPAN])]
            late[start : start + SPAN, :] = held[0]
        return held[0][start % SPAN : start % SPAN + TILE, :]

    finish_mirror(mirror_sums(columns, index[0:1, :], rates[...], total), index, rates, out)


def later_mirror_kernel(early, late, index, rates, out, total):
    def columns(i):
        start = i * TILE
        if start < early.shape[0]:
            return early[start : start + TILE, :]
        start -= early.shape[0]
        return late[start : start + TILE, :]

    finish_mirror(mirror_sums(columns, index[0:1, :], rates[...], total), index, rates, out)


def direct_kernel(early, late, index, got, out):
    patches = out.shape[1]
    rate = chosen(index[1:2, :], got[:, patches:, :]).astype(bf16)
    add = lax.broadcasted_iota(jnp.int32, (8, SPAN), 1) // TILE
    add = jnp.where(add == lax.broadcasted_iota(jnp.int32, (8, SPAN), 0), 1.0, 0.0).astype(bf16)
    rate = jnp.concatenate([rate] * (SPAN // TILE), axis=0)
    sums = [
        jnp.dot(add, turned[start : start + SPAN, :] * rate, preferred_element_type=f32)
        for turned in (early, late)
        for start in range(0, turned.shape[0], SPAN)
    ]
    sums = jnp.concatenate(sums, axis=0)
    out[...] = dropped(index[0:1, :], sums, out.shape[0] * patches).reshape(out.shape)


def step_body(stress, direct, got, rate_log, state, more, outs):
    normal_stress, rate_param, state_param, slip_length, self_stiffness, damping = (m[...] for m in more)
    rate_out, state_out, stress_out, *pushed_out = outs
    stress_rate = jnp.sum(direct[...].astype(f32), axis=0) + jnp.sum(
        got[:, : direct.shape[1], :].astype(f32), axis=0
    )
    speed = jnp.exp(rate_log)
    new_stress = stress + time_step * (stress_rate - self_stiffness * (speed - 1.0))
    new_state = state + time_step * (state_param / slip_length) * (jnp.exp(-state / state_param) - speed)
    new_rate = friction_solve(rate_log, new_stress, new_state, normal_stress, rate_param, damping)
    rate_out[...] = new_rate
    state_out[...] = new_state
    stress_out[...] = new_stress
    for out in pushed_out:
        pushed = (jnp.exp(new_rate) - 1.0).astype(bf16)
        out[...] = jnp.broadcast_to(pushed[None], out.shape)


def first_kernel(direct, got, log_rate, state, excess, *refs):
    more, outs = refs[:6], refs[6:]
    normal_stress, rate_param, damping = more[0][...], more[1][...], more[5][...]
    rate_log, begin = log_rate[...], state[...]
    ratio = 0.5 * jnp.exp(rate_log + begin / rate_param)
    balance = normal_stress * rate_param * jnp.log(ratio + jnp.sqrt(1.0 + ratio * ratio)) + damping * jnp.exp(
        rate_log
    )
    step_body(balance * (1.0 + excess[...]), direct, got, rate_log, begin, more, outs)


def later_kernel(direct, got, rate_log, state, stress, *refs):
    step_body(stress[...], direct, got, rate_log[...], state[...], refs[:6], refs[6:])


def call(kernel, out_shape, scratch=(), **kw):
    return pl.pallas_call(
        kernel,
        out_shape=out_shape,
        scratch_shapes=list(scratch),
        compiler_params=pltpu.CompilerParams(vmem_limit_bytes=24 << 20),
        **kw,
    )


def on_device(
    log_rate,
    state,
    excess,
    normal_stress,
    rate_param,
    state_param,
    slip_length,
    self_stiffness,
    damping,
    blocks,
    pattern,
    counts,
):
    patches = log_rate.shape[0]
    flat = (patches // LANES, LANES)
    row_count = lax.axis_size("row")
    col_count = lax.axis_size("col")
    slots, tile_size = blocks.shape[2:]
    shape = jax.ShapeDtypeStruct

    tiles = blocks.reshape(slots, tile_size)
    places = pattern.reshape(slots, 2).T
    more = [
        a.reshape(flat)
        for a in (normal_stress, rate_param, state_param, slip_length, self_stiffness, damping)
    ]
    rate_log = log_rate.reshape(flat)
    state = state.reshape(flat)
    stress = excess.reshape(flat)
    vmem = pl.BlockSpec(memory_space=pltpu.VMEM)
    hbm = pl.BlockSpec(memory_space=pltpu.HBM)

    def far(x):
        return pltpu.with_memory_space_constraint(x, pltpu.HBM)

    def exchange(x, axis):
        order = [k ^ ORDER[axis] for k in range(x.shape[0])]
        return lax.all_to_all(
            x, axis, split_axis=0, concat_axis=0, tiled=True, axis_index_groups=[order]
        )

    pushed = call(push_kernel, shape((col_count,) + flat, bf16), )(far(rate_log))
    begin = tile_size // 8 * 5

    def landing(lanes, copies):
        return (pltpu.VMEM((slots, lanes), bf16), pltpu.SemaphoreType.DMA((copies,)))

    early, index = call(
        functools.partial(turn_kernel, patches // TILE),
        (shape((begin, slots), bf16), shape((8, slots), jnp.int32)),
        landing(begin, slots // LANES) + (pltpu.VMEM((2, slots), jnp.int32), pltpu.SemaphoreType.DMA),
        in_specs=[hbm, hbm, pl.BlockSpec(memory_space=pltpu.SMEM)],
    )(far(tiles), far(places), counts)
    total = pltpu.VMEM((2, TILE, slots), f32)
    mixed_shape = shape((row_count, 2 * flat[0], LANES), bf16)
    for step_index in range(STEPS):
        row_rates = exchange(pushed, "col")
        if step_index:
            mixed = call(later_mirror_kernel, mixed_shape, (total,))(early, late, index, row_rates)
        else:
            mixed, late = call(
                first_mirror_kernel,
                (mixed_shape, shape((tile_size - begin, slots), bf16)),
                (total,) + landing(tile_size - begin, (tile_size - begin) // SPAN),
                in_specs=[hbm, vmem, vmem, vmem],
            )(far(tiles), early, index, row_rates)
        got = exchange(mixed, "row")
        direct = call(direct_kernel, shape((col_count,) + flat, bf16))(early, late, index, got)
        direct = exchange(direct, "col")
        outs = [shape(flat, f32)] * 3
        if step_index < STEPS - 1:
            outs.append(shape((col_count,) + flat, bf16))
        result = call(later_kernel if step_index else first_kernel, tuple(outs))(
            direct, got, rate_log, state, stress, *more
        )
        rate_log, state, stress = result[:3]
        pushed = result[-1]
    return tuple(a.reshape(patches) for a in (rate_log, state, stress))


def solution(mesh):
    in_specs = (P(("row", "col")),) * 9 + (
        P("row", "col", None, None),
        P("row", "col", None, None),
        P("row", "col"),
    )
    out_specs = (P(("row", "col")), P(("row", "col")), P(("row", "col")))
    return jax.shard_map(
        on_device, mesh=mesh, in_specs=in_specs, out_specs=out_specs, check_vma=False
    )
```
